32 devices in a mesh: src: 4 (over x, core), gy: 4 (over z), gx: 2 (over y).
Axes of the slice: x: 2, y: 2, z: 4, core: 2. Of those that a mesh axis runs over, the one named last changes fastest.
Arguments:
- fields: bfloat16 [5, 256, 256, 1024], P(None, 'src', 'gy', 'gx'), may hold values from -6 to 6
- dx_op: bfloat16 [1024, 1024], P(('gy', 'gx'))
- y_ops: bfloat16 [2, 256, 256], replicated
- dz_op: bfloat16 [256, 256], replicated
- metric_x: float32 [1024], P('gx'), may hold values from 0.5 to 2
- metric_y: float32 [256], P('gy'), may hold values from 0.5 to 2
- metric_z: float32 [256], P('src'), may hold values from 0.5 to 2
- mean_u: float32 [256, 256], P('src', 'gy'), may hold values from 0.2 to 1.5
- surface_rows: bfloat16 [256, 5, 256], P(('src', 'gy', 'gx')), may hold values from -6 to 6
- row_block: int32 [256], P(('src', 'gy', 'gx')), may hold values from 0 to 8191
- row_offsets: int32 [32, 9], P(('src', 'gy', 'gx')), may hold values from 0 to 8, as said below
Outputs:
- fields_next: bfloat16 [5, 256, 256, 1024], P(None, 'src', 'gy', 'gx')
The draws below stay inside these ranges and needn't reach their ends.
Inputs may be any that keep to these rules, and one draw needn't show every extreme that they name: row_offsets[d, 0] = 0 and row_offsets[d, 8] = 8; the offsets never fall; at most 2 rows of one device go to one destination, and in every draw some destination receives 2 rows from every device of its src index.
All inputs are finite; a program needn't handle non-finite values.
Results may differ from the reference program's by a relative error of at most 0.0049.
Values may be sent and summed in bfloat16 or wider, within the bound.
No kernel may reach another device: no remote copies, remote signals or barrier semaphores. Data moves between devices by JAX's collectives and lax.ppermute only.
A program may use at most 384 MiB of HBM per device.

```python
import math
import jax
import jax.numpy as jnp

NX = 1024
NY = 256
NZ = 256
ROW_LEN = 256
CAP = 2
NCOL = 8
ROWS_DEV = 8
ROWS = 256
CZ = 64
CY = 64
CX = 512
BLOCKS_DEV = 8192
N_GX = 2
DEVICES = 32


def base_noise(key, extent):
    noise = jax.random.normal(key, (extent, extent))
    return 0.6 * noise / math.sqrt(extent)


def derivative_matrix(noise, extent):
    near_band = 0.75 * (jnp.eye(extent, k=1) - jnp.eye(extent, k=-1))
    far_band = 0.15 * (jnp.eye(extent, k=2) - jnp.eye(extent, k=-2))
    return noise + near_band - far_band


def filter_matrix(noise, extent):
    return noise + 0.5 * jnp.eye(extent) + 0.25 * (jnp.eye(extent, k=1) + jnp.eye(extent, k=-1))


def draw_dx_op(key, part):
    return derivative_matrix(base_noise(jax.random.fold_in(key, 3), NX), NX).astype(jnp.bfloat16)


def draw_y_ops(key, part):
    deriv_matrix = derivative_matrix(base_noise(jax.random.fold_in(key, 5), NY), NY)
    smooth_matrix = filter_matrix(base_noise(jax.random.fold_in(key, 6), NY), NY)
    return jnp.stack([deriv_matrix, smooth_matrix]).astype(jnp.bfloat16)


def draw_dz_op(key, part):
    return derivative_matrix(base_noise(jax.random.fold_in(key, 7), NZ), NZ).astype(jnp.bfloat16)


def draw_row_offsets(key, part):
    groups = DEVICES // NCOL
    across = NX // CX
    scores = jax.random.randint(jax.random.fold_in(key, 11), (DEVICES, NCOL), 0, 256)
    hot_column = jax.random.randint(jax.random.fold_in(key, 12), (groups,), 0, NCOL)
    hot_device = jnp.repeat(hot_column, NCOL)
    columns = jnp.arange(NCOL, dtype=jnp.int32)
    in_band = (jnp.abs(columns[None, :] // across - (hot_device // across)[:, None]) <= 1).astype(jnp.int32)
    is_hot = (columns[None, :] == hot_device[:, None]).astype(jnp.int32)
    weighted = scores * 4 + 1024 * is_hot + 512 * in_band
    ranked = weighted * NCOL + columns[None, :]
    ordering = jnp.argsort(-ranked, axis=1)
    chosen = ordering[:, :NCOL // 2]
    picked = jnp.any(chosen[:, :, None] == columns[None, None, :], axis=1).astype(jnp.int32)
    counts = picked * CAP
    running = jnp.cumsum(counts, axis=1)
    return jnp.concatenate([jnp.zeros((DEVICES, 1), jnp.int32), running.astype(jnp.int32)], axis=1)


def plant(array, key, low, largest):
    place = [jax.random.randint(jax.random.fold_in(key, axis), (), 0, length) for axis, length in enumerate(array.shape)]
    widest = array.shape.index(max(array.shape))
    beside = place[:widest] + [(place[widest] + 1) % array.shape[widest]] + place[widest + 1:]
    return array.at[tuple(place)].set(low).at[tuple(beside)].set(largest)


def steps_of(own_key, shape, pieces, low, largest):
    level = 1.0
    for axis_at, blocks in pieces:
        steps = jax.random.uniform(jax.random.fold_in(jax.random.fold_in(own_key, 6), axis_at), (blocks,), jnp.float32, low / len(pieces), largest / len(pieces))
        level = level * jnp.repeat(jnp.exp(steps), shape[axis_at] // blocks).reshape((-1,) + (1,) * (len(shape) - 1 - axis_at))
    return level


def scatter_about(rng, dims, spread, reach, shards=(), kind=jnp.bfloat16):
    level = steps_of(rng, dims, shards, -0.22, 0.18) if shards else 1.0
    values = jax.random.normal(rng, dims, jnp.float32) * spread * level
    return jnp.minimum(jnp.maximum(values, -reach), reach).astype(kind)


def setup_inputs(seed: int = 0) -> dict:
    streams_of = jax.random.split(jax.random.key(seed), 12)
    fields = scatter_about(streams_of[0], (5, NZ, NY, NX), 1.0, 6.0, ((1, 4), (2, 4), (3, 2)))
    dx_op = draw_dx_op(jax.random.fold_in(streams_of[11], 71), 0)
    y_ops = draw_y_ops(jax.random.fold_in(streams_of[11], 71), 0)
    dz_op = draw_dz_op(jax.random.fold_in(streams_of[11], 71), 0)
    metric_x = jnp.clip(jnp.exp(math.log(2.0) - 1.3862944 * jax.random.uniform(streams_of[4], (NX,), jnp.float32) ** steps_of(streams_of[4], (NX,), ((0, 2),), -0.2, 0.2)), 0.5, 2.0)
    metric_y = jnp.clip(jnp.exp(math.log(2.0) - 1.3862944 * jax.random.uniform(streams_of[5], (NY,), jnp.float32) ** steps_of(streams_of[5], (NY,), ((0, 4),), -0.2, 0.2)), 0.5, 2.0)
    metric_z = jnp.clip(jnp.exp(math.log(2.0) - 1.3862944 * jax.random.uniform(streams_of[6], (NZ,), jnp.float32) ** steps_of(streams_of[6], (NZ,), ((0, 4),), -0.2, 0.2)), 0.5, 2.0)
    mean_u = jnp.clip(0.2 + 1.3 * jax.random.uniform(streams_of[7], (NZ, NY), jnp.float32) ** steps_of(streams_of[7], (NZ, NY), ((0, 4), (1, 4)), -0.2, 0.2), 0.2, 1.5)
    surface_rows = scatter_about(streams_of[8], (ROWS, 5, ROW_LEN), 1.0, 6.0, ((0, 32),))
    row_block = plant(jax.random.randint(streams_of[9], (ROWS,), 0, BLOCKS_DEV), jax.random.fold_in(streams_of[9], 1), 0, BLOCKS_DEV - 1).astype(jnp.int32)
    row_offsets = draw_row_offsets(jax.random.fold_in(streams_of[11], 71), 0)
    return {"fields": fields, "dx_op": dx_op, "y_ops": y_ops, "dz_op": dz_op, "metric_x": metric_x, "metric_y": metric_y, "metric_z": metric_z, "mean_u": mean_u, "surface_rows": surface_rows, "row_block": row_block, "row_offsets": row_offsets}


step_size = 0.25


def along_x(field, dx_op):
    flattened = jnp.dot(field.reshape(-1, NX), dx_op.T, preferred_element_type=jnp.float32)
    return flattened.reshape(NZ, NY, NX).astype(jnp.bfloat16)


def along_y(field, matrix):
    return jnp.einsum('zjx,ij->zix', field.astype(jnp.float32), matrix.astype(jnp.float32)).astype(jnp.bfloat16)


def along_z(field, dz_op):
    flattened = jnp.dot(dz_op, field.reshape(NZ, -1), preferred_element_type=jnp.float32)
    return flattened.reshape(NZ, NY, NX).astype(jnp.bfloat16)


def reference(fields, dx_op, y_ops, dz_op, metric_x, metric_y, metric_z, mean_u, surface_rows, row_block, row_offsets):
    scale_x = metric_x[None, None, :]
    scale_y = metric_y[None, :, None]
    scale_z = metric_z[:, None, None]
    speed = mean_u[:, :, None]
    slope_u = scale_x * along_x(fields[1], dx_op).astype(jnp.float32)
    slope_p = scale_x * along_x(fields[4], dx_op).astype(jnp.float32)
    grad_vy = scale_y * along_y(fields[2], y_ops[0]).astype(jnp.float32)
    grad_py = scale_y * along_y(fields[4], y_ops[0]).astype(jnp.float32)
    grad_wz = scale_z * along_z(fields[3], dz_op).astype(jnp.float32)
    grad_pz = scale_z * along_z(fields[4], dz_op).astype(jnp.float32)
    divergence = slope_u + grad_vy + grad_wz
    row_ids = jnp.arange(ROWS, dtype=jnp.int32)
    device = row_ids // ROWS_DEV
    position = row_ids % ROWS_DEV
    bounds = row_offsets[device, 1:]
    column = jnp.sum((position[:, None] >= bounds).astype(jnp.int32), axis=1)
    owner_group = device // NCOL
    owner_row = column // N_GX
    owner_col = column % N_GX
    cell_ids = row_block[:, None] * ROW_LEN + jnp.arange(ROW_LEN, dtype=jnp.int32)[None, :]
    local_z = cell_ids // (CY * CX)
    local_y = (cell_ids // CX) % CY
    local_x = cell_ids % CX
    target = ((owner_group[:, None] * CZ + local_z) * NY + owner_row[:, None] * CY + local_y) * NX + owner_col[:, None] * CX + local_x
    target = target.reshape(-1).astype(jnp.int32)
    results = []
    for variable in range(5):
        if variable == 1:
            slope_x = slope_u
        elif variable == 4:
            slope_x = slope_p
        else:
            slope_x = scale_x * along_x(fields[variable], dx_op).astype(jnp.float32)
        if variable == 0:
            change = -(speed * slope_x + divergence)
        elif variable == 1:
            change = -(speed * slope_x + slope_p)
        elif variable == 2:
            change = -(speed * slope_x + grad_py)
        elif variable == 3:
            change = -(speed * slope_x + grad_pz)
        else:
            change = -(speed * slope_x + divergence)
        filtered = along_y(fields[variable], y_ops[1]).astype(jnp.float32)
        added = jnp.zeros((NZ * NY * NX,), jnp.float32).at[target].add(surface_rows[:, variable, :].astype(jnp.float32).reshape(-1))
        combined = filtered + step_size * change + added.reshape(NZ, NY, NX)
        results.append(combined.astype(jnp.bfloat16))
    return jnp.stack(results)
```

```python
import math

import jax
import jax.numpy as jnp
from jax import lax
from jax.experimental import pallas as pl
from jax.experimental.pallas import tpu as pltpu
from jax.sharding import PartitionSpec as P

ROW_LEN = 256
CAP = 2
DIGIT = 128
SLAB = 16
STEP_SIZE = 0.25
IN_ORDER = (2, 0, 4, 1, 3)
OUT_ORDER = (0, 2, 4, 1, 3)
Y_TERM = {0: 2, 2: 4, 4: 2}


class Axis:
    def __init__(self, name):
        self.name = name
        self.size = lax.axis_size(name)
        self.me = lax.axis_index(name)
        self.xor = self.size & (self.size - 1) == 0

    def dest(self, k):
        return jnp.bitwise_xor(self.me, k) if self.xor else (self.me + k) % self.size

    def source(self, k):
        return jnp.bitwise_xor(self.me, k) if self.xor else (self.me - k) % self.size

    def send(self, array, k):
        pairs = [(i, i ^ k if self.xor else (i + k) % self.size) for i in range(self.size)]
        return lax.ppermute(array, self.name, pairs)

    def gather(self, array):
        return [array] + [self.send(array, k) for k in range(1, self.size)]

    def steps(self):
        return jnp.arange(self.size, dtype=jnp.int32)

    def in_place_order(self, pieces):
        return jnp.take(jnp.stack(pieces), self.source(self.steps()), axis=0)


def cost(flops, bytes_accessed):
    return pl.CostEstimate(flops=int(flops), transcendentals=0, bytes_accessed=int(bytes_accessed))


def largest_divisor(extent, most):
    return max(d for d in range(1, min(extent, most) + 1) if extent % d == 0)


def y_part(own, other, matrices, scale, name):
    num = len(own)
    planes, rows, cells = own[0].shape
    zb = largest_divisor(planes, 4)
    extent = num * rows
    full = jax.ShapeDtypeStruct(own[0].shape, jnp.bfloat16)

    def kernel(*refs):
        own_refs = refs[:num]
        other_refs = refs[num : num + len(other)]
        mats_ref, scale_ref = refs[num + len(other) : num + len(other) + 2]
        out_refs = refs[num + len(other) + 2 :]
        for z in range(zb):
            lines = jnp.concatenate([r[z] for r in own_refs], axis=0)
            acc = jnp.dot(mats_ref[1], lines, preferred_element_type=jnp.float32)
            if other_refs:
                lines = jnp.concatenate([r[z] for r in other_refs], axis=0)
                acc += scale_ref[...] * jnp.dot(mats_ref[0], lines, preferred_element_type=jnp.float32)
            for k in range(num):
                out_refs[k][z] = acc[k * rows : (k + 1) * rows].astype(jnp.bfloat16)

    block = pl.BlockSpec((zb, rows, cells), lambda i: (i, 0, 0))
    total = len(own) + len(other)
    return pl.pallas_call(
        kernel,
        grid=(planes // zb,),
        in_specs=[block] * total
        + [
            pl.BlockSpec((2, extent, extent), lambda i: (0, 0, 0)),
            pl.BlockSpec((extent, 1), lambda i: (0, 0)),
        ],
        out_specs=[block] * num,
        out_shape=[full] * num,
        name=name,
        cost_estimate=cost(
            2 * extent * extent * planes * cells * (total // num),
            2 * extent * planes * cells * (total // num + 1),
        ),
    )(*own, *other, matrices, scale)


def z_part(fields, arrived, operator, scale):
    _, planes, rows, cells = fields.shape
    num = len(arrived) + 1
    slab = largest_divisor(rows, SLAB)
    size = planes * slab

    def kernel(own_ref, *refs):
        in_refs = (own_ref,) + refs[: num - 1]
        op_ref, scale_ref, out_ref = refs[num - 1 :]
        acc = jnp.zeros((size, cells), jnp.float32)
        for k in range(num):
            acc += jnp.dot(op_ref[k], in_refs[k][0].reshape(size, cells), preferred_element_type=jnp.float32)
        out_ref[0] = (scale_ref[...] * acc).reshape(planes, slab, cells).astype(jnp.bfloat16)

    block = (1, planes, slab, cells)
    here = pl.BlockSpec(block, lambda a, i: (a, 0, i, 0))
    return pl.pallas_call(
        kernel,
        grid=(2, rows // slab),
        in_specs=[pl.BlockSpec(block, lambda a, i: (a + 3, 0, i, 0))]
        + [here] * (num - 1)
        + [
            pl.BlockSpec((num, size, size), lambda a, i: (0, 0, 0)),
            pl.BlockSpec((size, 1), lambda a, i: (0, 0)),
        ],
        out_specs=here,
        out_shape=jax.ShapeDtypeStruct((2, planes, rows, cells), jnp.bfloat16),
        name="z_part",
        cost_estimate=cost(
            4 * num * size * size * cells * (rows // slab), 4 * (num + 1) * planes * rows * cells
        ),
    )(fields, *arrived, operator, scale)


def x_part(fields, arrived, operator, scale_x, speed, z_terms, rows_in, targets):
    num_vars, planes, rows, cells = fields.shape
    num = len(arrived) + 1
    zb = largest_divisor(planes, max(1, 256 // rows))
    size = zb * rows
    num_rows = targets.shape[0]
    width = min(ROW_LEN, cells)

    def kernel(targets_ref, own_ref, *refs):
        in_refs = (own_ref,) + refs[: num - 1]
        op_ref, scale_ref, speed_ref, z_ref, rows_ref, out_ref = refs[num - 1 :]
        speed_col = speed_ref[...].reshape(size, 1)

        def slope(v):
            acc = jnp.dot(
                in_refs[0][v].reshape(size, cells), op_ref[0], preferred_element_type=jnp.float32
            )
            for k in range(1, num):
                acc += jnp.dot(
                    in_refs[k][v].reshape(size, cells), op_ref[k], preferred_element_type=jnp.float32
                )
            return acc * scale_ref[...]

        def z_term(a):
            return z_ref[a].reshape(size, cells).astype(jnp.float32)

        def put(v, value):
            out_ref[v] = (-STEP_SIZE * value).reshape(zb, rows, cells)

        slope_u = slope(1)
        slope_p = slope(4)
        divergence = slope_u + z_term(0)
        put(1, speed_col * slope_u + slope_p)
        put(4, speed_col * slope_p + divergence)
        put(0, speed_col * slope(0) + divergence)
        put(2, speed_col * slope(2))
        put(3, speed_col * slope(3) + z_term(1))
        first = pl.program_id(0) * zb

        @pl.loop(0, num_rows)
        def _(r):
            for piece in range(ROW_LEN // width):
                cell = targets_ref[r] * ROW_LEN + piece * width
                plane = cell // (rows * cells) - first

                @pl.when((plane >= 0) & (plane < zb))
                def _():
                    row = (cell // cells) % rows
                    start = pl.multiple_of(cell % cells, width)
                    for v in range(num_vars):
                        place = (v, plane, pl.ds(row, 1), pl.ds(start, width))
                        out_ref[place] += rows_ref[r, v : v + 1, piece * width : (piece + 1) * width]

    block = pl.BlockSpec((num_vars, zb, rows, cells), lambda i, t: (0, i, 0, 0))
    return pl.pallas_call(
        kernel,
        grid_spec=pltpu.PrefetchScalarGridSpec(
            num_scalar_prefetch=1,
            grid=(planes // zb,),
            in_specs=[block] * num
            + [
                pl.BlockSpec((num, cells, cells), lambda i, t: (0, 0, 0)),
                pl.BlockSpec((1, cells), lambda i, t: (0, 0)),
                pl.BlockSpec((zb, rows, 1), lambda i, t: (i, 0, 0)),
                pl.BlockSpec((2, zb, rows, cells), lambda i, t: (0, i, 0, 0)),
                pl.BlockSpec(rows_in.shape, lambda i, t: (0, 0, 0)),
            ],
            out_specs=block,
        ),
        out_shape=jax.ShapeDtypeStruct(fields.shape, jnp.float32),
        name="x_part",
        cost_estimate=cost(
            2 * num_vars * planes * rows * cells * cells * num,
            num_vars * planes * rows * cells * (2 * num + 5),
        ),
    )(targets, fields, *arrived, operator, scale_x, speed, z_terms, rows_in)


def finish(total, rest, part, variable, place, name):
    planes, rows, cells = part.shape
    zb = largest_divisor(planes, 8)
    per = planes // zb

    def kernel(place_ref, rest_ref, part_ref, *refs):
        refs[-1][0] = (rest_ref[0] + part_ref[...].astype(jnp.float32)).astype(jnp.bfloat16)

    big = pl.BlockSpec((1, zb, rows, cells), lambda i, p: (variable, p[0] * per + i, 0, 0))
    in_specs = [big, pl.BlockSpec((zb, rows, cells), lambda i, p: (i, 0, 0))]
    operands = [rest, part]
    aliases = {}
    if total is not None:
        in_specs.append(pl.BlockSpec(memory_space=pl.ANY))
        operands.append(total)
        aliases = {3: 0}
    return pl.pallas_call(
        kernel,
        grid_spec=pltpu.PrefetchScalarGridSpec(
            num_scalar_prefetch=1, grid=(per,), in_specs=in_specs, out_specs=big
        ),
        out_shape=jax.ShapeDtypeStruct(rest.shape, jnp.bfloat16),
        input_output_aliases=aliases,
        name=name,
        cost_estimate=cost(planes * rows * cells, 8 * planes * rows * cells),
    )(place, *operands)


def route_rows(gy, gx, surface_rows, row_block, row_offsets, num_blocks):
    num_vars = surface_rows.shape[1]
    starts = row_offsets[0, :-1]
    counts = row_offsets[0, 1:] - starts
    slots = jnp.arange(CAP, dtype=jnp.int32)
    is_valid = slots[None, :] < counts[:, None]
    row_index = jnp.where(is_valid, starts[:, None] + slots[None, :], 0).reshape(-1)
    valid = is_valid.reshape(-1)[:, None]
    picked = jnp.take(surface_rows.reshape(-1, num_vars * ROW_LEN), row_index, axis=0)
    picked = jnp.where(valid, picked, jnp.zeros((), jnp.bfloat16))
    blocks = jnp.where(is_valid.reshape(-1), jnp.take(row_block, row_index), 0)
    digits = []
    scale = 1
    while scale < num_blocks:
        digits.append((blocks // scale) % DIGIT)
        scale *= DIGIT
    tail = jnp.stack(digits, axis=1).astype(jnp.bfloat16)
    tail = jnp.pad(tail, ((0, 0), (0, -len(digits) % 128)))
    packed = jnp.concatenate([picked, tail], axis=1).reshape(gy.size, gx.size, CAP, -1)
    for axis in (gy, gx):
        by_dest = [lax.dynamic_index_in_dim(packed, axis.dest(k), 0, keepdims=False) for k in range(axis.size)]
        got = [by_dest[0]] + [axis.send(by_dest[k], k) for k in range(1, axis.size)]
        packed = jnp.stack(got, axis=1) if axis is gy else jnp.stack(got)
    flat = packed.reshape(-1, packed.shape[-1])
    rows_in = flat[:, : num_vars * ROW_LEN].astype(jnp.float32).reshape(-1, num_vars, ROW_LEN)
    targets = jnp.zeros((flat.shape[0],), jnp.int32)
    for place in range(len(digits)):
        digit = flat[:, num_vars * ROW_LEN + place].astype(jnp.float32).astype(jnp.int32)
        targets += digit * DIGIT**place
    return rows_in, targets


def x_operator(src, gy, gx, dx_op):
    rows, extent = dx_op.shape
    cells = rows * gy.size
    share = rows // src.size if rows % src.size == 0 else rows
    split = share != rows
    piece = lax.dynamic_slice_in_dim(dx_op, src.me * share, share, 0) if split else dx_op
    columns = gy.in_place_order(gy.gather(piece))
    blocks = gx.in_place_order(gx.gather(columns)).swapaxes(0, 1)
    blocks = blocks.reshape(gy.size * gx.size, share, extent)
    needed = lax.dynamic_slice_in_dim(blocks, gx.me * gy.size, gy.size, 0)
    if split:
        needed = src.in_place_order(src.gather(needed)).swapaxes(0, 1)
    turned = needed.reshape(cells, extent).T.reshape(gx.size, cells, cells)
    return jnp.take(turned, gx.source(gx.steps()), axis=0)


def z_operator(src, dz_op, planes, slab):
    own = lax.dynamic_slice_in_dim(dz_op, src.me * planes, planes, 0)
    blocks = own.reshape(planes, src.size, planes).swapaxes(0, 1)
    blocks = jnp.take(blocks, src.source(src.steps()), axis=0)
    size = planes * slab
    index = jnp.arange(size, dtype=jnp.int32)
    spread = (index[:, None] // slab == jnp.arange(planes, dtype=jnp.int32)[None, :]).astype(jnp.bfloat16)
    same_row = (index[:, None] % slab) == (index[None, :] % slab)
    wide = jnp.einsum("pi,kij->kpj", spread, blocks, preferred_element_type=jnp.float32).astype(jnp.bfloat16)
    wide = jnp.einsum("kpj,qj->kpq", wide, spread, preferred_element_type=jnp.float32).astype(jnp.bfloat16)
    return jnp.where(same_row[None], wide, jnp.zeros((), jnp.bfloat16))


def y_operator(gy, y_ops, rows):
    num = y_ops.shape[0]
    blocks = y_ops.reshape(num, gy.size, rows, gy.size, rows)
    blocks = jnp.take(blocks, gy.dest(gy.steps()), axis=1)
    blocks = jnp.take(blocks, gy.source(gy.steps()), axis=3)
    return blocks.reshape(y_ops.shape)


def on_device(
    fields,
    dx_op,
    y_ops,
    dz_op,
    metric_x,
    metric_y,
    metric_z,
    mean_u,
    surface_rows,
    row_block,
    row_offsets,
):
    num_vars, planes, rows, cells = fields.shape
    src, gy, gx = Axis("src"), Axis("gy"), Axis("gx")
    share = planes // gy.size

    held = {}

    def exchange(blocks):
        return [blocks[0]] + [gy.send(blocks[k], k) for k in range(1, gy.size)]

    started = []
    for v in IN_ORDER:
        blocks = [
            lax.dynamic_slice(fields, (v, gy.dest(k) * share, 0, 0), (1, share, rows, cells))[0]
            for k in range(gy.size)
        ]
        if len(started) >= 2:
            blocks, _ = lax.optimization_barrier((blocks, held[started[-2]]))
        held[v] = exchange(blocks)
        started.append(v)

    x_arrived = [gx.send(fields, k) for k in range(1, gx.size)]
    z_fields = fields[3:5]
    z_arrived = [src.send(z_fields, k) for k in range(1, src.size)]

    matrices = y_operator(gy, y_ops, rows)
    metric_all = gy.in_place_order(gy.gather(metric_y.reshape(1, rows)))
    scale_y = -STEP_SIZE * jnp.take(metric_all, gy.dest(gy.steps()), axis=0).reshape(-1, 1)

    parts = {}
    sent = []
    for v in OUT_ORDER:
        other = held[Y_TERM[v]] if v in Y_TERM else []
        blocks = y_part(held[v], other, matrices, scale_y, f"y_part{v}")
        if len(sent) >= 2:
            blocks, _ = lax.optimization_barrier((blocks, parts[sent[-2]]))
        parts[v] = exchange(blocks)
        sent.append(v)

    slab = largest_divisor(rows, SLAB)
    z_scale = jnp.repeat(metric_z, slab).reshape(-1, 1)
    z_terms = z_part(fields, z_arrived, z_operator(src, dz_op, planes, slab), z_scale)
    num_blocks = planes * rows * cells // ROW_LEN
    rows_in, targets = route_rows(gy, gx, surface_rows, row_block, row_offsets, num_blocks)
    rest = x_part(
        fields,
        x_arrived,
        x_operator(src, gy, gx, dx_op),
        metric_x.reshape(1, cells),
        mean_u.reshape(planes, rows, 1),
        z_terms,
        rows_in,
        targets,
    )
    total = None
    for v in OUT_ORDER:
        for k in range(gy.size):
            place = gy.source(k).reshape(1).astype(jnp.int32)
            total = finish(total, rest, parts[v][k], v, place, f"finish{v}_{k}")
    return total


def solution(mesh):
    return jax.shard_map(
        on_device,
        mesh=mesh,
        in_specs=(
            P(None, "src", "gy", "gx"),
            P(("gy", "gx"), None),
            P(),
            P(),
            P("gx"),
            P("gy"),
            P("src"),
            P("src", "gy"),
            P(("src", "gy", "gx"), None, None),
            P(("src", "gy", "gx")),
            P(("src", "gy", "gx"), None),
        ),
        out_specs=P(None, "src", "gy", "gx"),
        check_vma=False,
    )
```

```python
import jax
import jax.numpy as jnp
from jax import lax
from jax.experimental import pallas as pl
from jax.experimental.pallas import tpu as pltpu
from jax.sharding import PartitionSpec as P


ROW_LEN = 256
CAP = 2
DIGIT = 128
SLAB = 16
STEP_SIZE = 0.25
Y_ITEMS = (
    ("in", 2),
    ("in", 0),
    ("in", 4),
    ("in", 1),
    ("out", 0),
    ("in", 3),
    ("out", 2),
    ("out", 4),
    ("out", 1),
    ("out", 3),
)
IN_FLIGHT = 3
AFTER_REST = 1
AFTER_FIRST = 3
Y_TERM = {0: 2, 2: 4, 4: 2}


class Axis:
    def __init__(self, name):
        self.name = name
        self.size = lax.axis_size(name)
        self.me = lax.axis_index(name)
        self.xor = self.size & (self.size - 1) == 0

    def dest(self, k):
        return jnp.bitwise_xor(self.me, k) if self.xor else (self.me + k) % self.size

    def source(self, k):
        return jnp.bitwise_xor(self.me, k) if self.xor else (self.me - k) % self.size

    def send(self, array, k):
        pairs = [(i, i ^ k if self.xor else (i + k) % self.size) for i in range(self.size)]
        return lax.ppermute(array, self.name, pairs)

    def gather(self, array):
        return [array] + [self.send(array, k) for k in range(1, self.size)]

    def steps(self):
        return jnp.arange(self.size, dtype=jnp.int32)

    def in_place_order(self, pieces):
        return jnp.take(jnp.stack(pieces), self.source(self.steps()), axis=0)


def cost(flops, bytes_accessed):
    return pl.CostEstimate(flops=int(flops), transcendentals=0, bytes_accessed=int(bytes_accessed))


def largest_divisor(extent, most):
    return max(d for d in range(1, min(extent, most) + 1) if extent % d == 0)


def y_part(fields, place, variable, arrived, term, term_arrived, matrices, scale):
    num = len(arrived) + 1
    planes, rows, cells = arrived[0].shape
    zb = largest_divisor(planes, 4)
    per = planes // zb
    extent = num * rows
    full = jax.ShapeDtypeStruct(arrived[0].shape, jnp.bfloat16)
    groups = [(variable, arrived)] + ([] if term is None else [(term, term_arrived)])
    total = num * len(groups)

    def kernel(place_ref, *refs):
        mats_ref, scale_ref = refs[total : total + 2]
        out_refs = refs[total + 2 :]

        def product(group, matrix, z):
            first, *others = refs[group * num : (group + 1) * num]
            lines = jnp.concatenate([first[0, z]] + [r[z] for r in others], axis=0)
            return jnp.dot(mats_ref[matrix], lines, preferred_element_type=jnp.float32)

        for z in range(zb):
            acc = product(0, 1, z)
            if term is not None:
                acc += scale_ref[...] * product(1, 0, z)
            for k in range(num):
                out_refs[k][z] = acc[k * rows : (k + 1) * rows].astype(jnp.bfloat16)

    def own_place(v):
        return lambda i, p: (v, p[0] * per + i, 0, 0)

    block = pl.BlockSpec((zb, rows, cells), lambda i, p: (i, 0, 0))
    in_specs = []
    operands = []
    for v, blocks in groups:
        in_specs += [pl.BlockSpec((1, zb, rows, cells), own_place(v))] + [block] * (num - 1)
        operands += [fields] + list(blocks)
    in_specs += [
        pl.BlockSpec((2, extent, extent), lambda i, p: (0, 0, 0)),
        pl.BlockSpec((extent, 1), lambda i, p: (0, 0)),
    ]
    return pl.pallas_call(
        kernel,
        grid_spec=pltpu.PrefetchScalarGridSpec(
            num_scalar_prefetch=1, grid=(per,), in_specs=in_specs, out_specs=[block] * num
        ),
        out_shape=[full] * num,
        cost_estimate=cost(
            2 * extent * extent * planes * cells * len(groups),
            2 * extent * planes * cells * (len(groups) + 1),
        ),
    )(place, *operands, matrices, scale)


def z_part(fields, arrived, operator, scale):
    _, planes, rows, cells = fields.shape
    num = len(arrived) + 1
    slab = largest_divisor(rows, SLAB)
    size = planes * slab

    def kernel(own_ref, *refs):
        in_refs = (own_ref,) + refs[: num - 1]
        op_ref, scale_ref, out_ref = refs[num - 1 :]
        acc = jnp.zeros((size, cells), jnp.float32)
        for k in range(num):
            acc += jnp.dot(op_ref[k], in_refs[k][0].reshape(size, cells), preferred_element_type=jnp.float32)
        out_ref[0] = (scale_ref[...] * acc).reshape(planes, slab, cells).astype(jnp.bfloat16)

    block = (1, planes, slab, cells)
    here = pl.BlockSpec(block, lambda a, i: (a, 0, i, 0))
    return pl.pallas_call(
        kernel,
        grid=(2, rows // slab),
        in_specs=[pl.BlockSpec(block, lambda a, i: (a + 3, 0, i, 0))]
        + [here] * (num - 1)
        + [
            pl.BlockSpec((num, size, size), lambda a, i: (0, 0, 0)),
            pl.BlockSpec((size, 1), lambda a, i: (0, 0)),
        ],
        out_specs=here,
        out_shape=jax.ShapeDtypeStruct((2, planes, rows, cells), jnp.bfloat16),
        name="z_part",
        cost_estimate=cost(
            4 * num * size * size * cells * (rows // slab), 4 * (num + 1) * planes * rows * cells
        ),
    )(fields, *arrived, operator, scale)


def x_part(fields, arrived, operator, scale_x, speed, z_terms, rows_in, targets):
    num_vars, planes, rows, cells = fields.shape
    num = len(arrived) + 1
    zb = largest_divisor(planes, max(1, 256 // rows))
    size = zb * rows
    num_rows = targets.shape[0]
    width = min(ROW_LEN, cells)

    def kernel(targets_ref, own_ref, *refs):
        in_refs = (own_ref,) + refs[: num - 1]
        op_ref, scale_ref, speed_ref, z_ref, rows_ref, out_ref = refs[num - 1 :]
        speed_col = speed_ref[...].reshape(size, 1)

        def slope(v):
            acc = jnp.dot(
                in_refs[0][v].reshape(size, cells), op_ref[0], preferred_element_type=jnp.float32
            )
            for k in range(1, num):
                acc += jnp.dot(
                    in_refs[k][v].reshape(size, cells), op_ref[k], preferred_element_type=jnp.float32
                )
            return acc * scale_ref[...]

        def z_term(a):
            return z_ref[a].reshape(size, cells).astype(jnp.float32)

        def put(v, value):
            out_ref[v] = (-STEP_SIZE * value).reshape(zb, rows, cells)

        slope_u = slope(1)
        slope_p = slope(4)
        divergence = slope_u + z_term(0)
        put(1, speed_col * slope_u + slope_p)
        put(4, speed_col * slope_p + divergence)
        put(0, speed_col * slope(0) + divergence)
        put(2, speed_col * slope(2))
        put(3, speed_col * slope(3) + z_term(1))
        first = pl.program_id(0) * zb

        @pl.loop(0, num_rows)
        def _(r):
            for piece in range(ROW_LEN // width):
                cell = targets_ref[r] * ROW_LEN + piece * width
                plane = cell // (rows * cells) - first

                @pl.when((plane >= 0) & (plane < zb))
                def _():
                    row = (cell // cells) % rows
                    start = pl.multiple_of(cell % cells, width)
                    for v in range(num_vars):
                        place = (v, plane, pl.ds(row, 1), pl.ds(start, width))
                        out_ref[place] += rows_ref[r, v : v + 1, piece * width : (piece + 1) * width]

    block = pl.BlockSpec((num_vars, zb, rows, cells), lambda i, t: (0, i, 0, 0))
    return pl.pallas_call(
        kernel,
        grid_spec=pltpu.PrefetchScalarGridSpec(
            num_scalar_prefetch=1,
            grid=(planes // zb,),
            in_specs=[block] * num
            + [
                pl.BlockSpec((num, cells, cells), lambda i, t: (0, 0, 0)),
                pl.BlockSpec((1, cells), lambda i, t: (0, 0)),
                pl.BlockSpec((zb, rows, 1), lambda i, t: (i, 0, 0)),
                pl.BlockSpec((2, zb, rows, cells), lambda i, t: (0, i, 0, 0)),
                pl.BlockSpec(rows_in.shape, lambda i, t: (0, 0, 0)),
            ],
            out_specs=block,
        ),
        out_shape=jax.ShapeDtypeStruct(fields.shape, jnp.float32),
        name="x_part",
        cost_estimate=cost(
            2 * num_vars * planes * rows * cells * cells * num,
            num_vars * planes * rows * cells * (2 * num + 5),
        ),
    )(targets, fields, *arrived, operator, scale_x, speed, z_terms, rows_in)


def finish(total, rest, part, variable, place):
    planes, rows, cells = part.shape
    zb = largest_divisor(planes, 8)
    per = planes // zb

    def kernel(place_ref, rest_ref, part_ref, *refs):
        refs[-1][0] = (rest_ref[0] + part_ref[...].astype(jnp.float32)).astype(jnp.bfloat16)

    big = pl.BlockSpec((1, zb, rows, cells), lambda i, p: (variable, p[0] * per + i, 0, 0))
    in_specs = [big, pl.BlockSpec((zb, rows, cells), lambda i, p: (i, 0, 0))]
    operands = [rest, part]
    aliases = {}
    if total is not None:
        in_specs.append(pl.BlockSpec(memory_space=pl.ANY))
        operands.append(total)
        aliases = {3: 0}
    return pl.pallas_call(
        kernel,
        grid_spec=pltpu.PrefetchScalarGridSpec(
            num_scalar_prefetch=1, grid=(per,), in_specs=in_specs, out_specs=big
        ),
        out_shape=jax.ShapeDtypeStruct(rest.shape, jnp.bfloat16),
        input_output_aliases=aliases,
        cost_estimate=cost(planes * rows * cells, 8 * planes * rows * cells),
    )(place, *operands)


def route_rows(gy, gx, surface_rows, row_block, row_offsets, num_blocks):
    num_vars = surface_rows.shape[1]
    starts = row_offsets[0, :-1]
    counts = row_offsets[0, 1:] - starts
    slots = jnp.arange(CAP, dtype=jnp.int32)
    is_valid = slots[None, :] < counts[:, None]
    row_index = jnp.where(is_valid, starts[:, None] + slots[None, :], 0).reshape(-1)
    valid = is_valid.reshape(-1)[:, None]
    picked = jnp.take(surface_rows.reshape(-1, num_vars * ROW_LEN), row_index, axis=0)
    picked = jnp.where(valid, picked, jnp.zeros((), jnp.bfloat16))
    blocks = jnp.where(is_valid.reshape(-1), jnp.take(row_block, row_index), 0)
    digits = []
    scale = 1
    while scale < num_blocks:
        digits.append((blocks // scale) % DIGIT)
        scale *= DIGIT
    tail = jnp.stack(digits, axis=1).astype(jnp.bfloat16)
    tail = jnp.pad(tail, ((0, 0), (0, -len(digits) % 128)))
    packed = jnp.concatenate([picked, tail], axis=1).reshape(gy.size, gx.size, CAP, -1)
    for axis in (gy, gx):
        by_dest = [lax.dynamic_index_in_dim(packed, axis.dest(k), 0, keepdims=False) for k in range(axis.size)]
        got = [by_dest[0]] + [axis.send(by_dest[k], k) for k in range(1, axis.size)]
        packed = jnp.stack(got, axis=1) if axis is gy else jnp.stack(got)
    flat = packed.reshape(-1, packed.shape[-1])
    rows_in = flat[:, : num_vars * ROW_LEN].astype(jnp.float32).reshape(-1, num_vars, ROW_LEN)
    targets = jnp.zeros((flat.shape[0],), jnp.int32)
    for place in range(len(digits)):
        digit = flat[:, num_vars * ROW_LEN + place].astype(jnp.float32).astype(jnp.int32)
        targets += digit * DIGIT**place
    return rows_in, targets


def x_operator(src, gy, gx, dx_op):
    rows, extent = dx_op.shape
    cells = rows * gy.size
    share = rows // src.size if rows % src.size == 0 else rows
    split = share != rows
    piece = lax.dynamic_slice_in_dim(dx_op, src.me * share, share, 0) if split else dx_op
    columns = gy.in_place_order(gy.gather(piece))
    blocks = gx.in_place_order(gx.gather(columns)).swapaxes(0, 1)
    blocks = blocks.reshape(gy.size * gx.size, share, extent)
    needed = lax.dynamic_slice_in_dim(blocks, gx.me * gy.size, gy.size, 0)
    if split:
        needed = src.in_place_order(src.gather(needed)).swapaxes(0, 1)
    turned = needed.reshape(cells, extent).T.reshape(gx.size, cells, cells)
    return jnp.take(turned, gx.source(gx.steps()), axis=0)


def z_operator(src, dz_op, planes, slab):
    own = lax.dynamic_slice_in_dim(dz_op, src.me * planes, planes, 0)
    blocks = own.reshape(planes, src.size, planes).swapaxes(0, 1)
    blocks = jnp.take(blocks, src.source(src.steps()), axis=0)
    size = planes * slab
    index = jnp.arange(size, dtype=jnp.int32)
    spread = (index[:, None] // slab == jnp.arange(planes, dtype=jnp.int32)[None, :]).astype(jnp.bfloat16)
    same_row = (index[:, None] % slab) == (index[None, :] % slab)
    wide = jnp.einsum("pi,kij->kpj", spread, blocks, preferred_element_type=jnp.float32).astype(jnp.bfloat16)
    wide = jnp.einsum("kpj,qj->kpq", wide, spread, preferred_element_type=jnp.float32).astype(jnp.bfloat16)
    return jnp.where(same_row[None], wide, jnp.zeros((), jnp.bfloat16))


def y_operator(gy, y_ops, rows):
    num = y_ops.shape[0]
    blocks = y_ops.reshape(num, gy.size, rows, gy.size, rows)
    blocks = jnp.take(blocks, gy.dest(gy.steps()), axis=1)
    blocks = jnp.take(blocks, gy.source(gy.steps()), axis=3)
    return blocks.reshape(y_ops.shape)


def on_device(
    fields,
    dx_op,
    y_ops,
    dz_op,
    metric_x,
    metric_y,
    metric_z,
    mean_u,
    surface_rows,
    row_block,
    row_offsets,
):
    _, planes, rows, cells = fields.shape
    src, gy, gx = Axis("src"), Axis("gy"), Axis("gx")
    share = planes // gy.size

    after = lax.optimization_barrier
    place = gy.me.reshape(1).astype(jnp.int32)

    def z_block(array, v, k):
        return lax.dynamic_slice(array, (v, gy.dest(k) * share, 0, 0), (1, share, rows, cells))[0]

    matrices = y_operator(gy, y_ops, rows)
    metric_all = gy.in_place_order(gy.gather(metric_y.reshape(1, rows)))
    scale_y = -STEP_SIZE * jnp.take(metric_all, gy.dest(gy.steps()), axis=0).reshape(-1, 1)
    slab = largest_divisor(rows, SLAB)
    z_scale = jnp.repeat(metric_z, slab).reshape(-1, 1)
    num_blocks = planes * rows * cells // ROW_LEN
    rows_in, targets = route_rows(gy, gx, surface_rows, row_block, row_offsets, num_blocks)
    turned = x_operator(src, gy, gx, dx_op)

    x_fields, *_ = after((fields, turned, rows_in))
    x_arrived = [gx.send(x_fields, k) for k in range(1, gx.size)]
    z_fields, _ = after((fields, turned))
    z_arrived = [src.send(z_fields[3:5], k) for k in range(1, src.size)]
    z_terms = z_part(fields, z_arrived, z_operator(src, dz_op, planes, slab), z_scale)
    rest = x_part(
        fields,
        x_arrived,
        turned,
        metric_x.reshape(1, cells),
        mean_u.reshape(planes, rows, 1),
        z_terms,
        rows_in,
        targets,
    )

    def finish_variable(total, v):
        for k in range(gy.size):
            at = gy.source(k).reshape(1).astype(jnp.int32)
            total = finish(total, rest, parts[v][k], v, at)
        return total

    held, parts, done = {}, {}, []
    total = None
    finished = []
    blocks = None
    for kind, v in Y_ITEMS:
        behind = done[-IN_FLIGHT] if len(done) >= IN_FLIGHT else None
        if kind == "in":
            source = fields
            if behind is not None or blocks is not None:
                source, _ = after((fields, blocks if behind is None else behind))
            blocks = {}
            for k in step_order(gy.size):
                blocks[k] = z_block(source, v, k)
                if not done and len(blocks) == 1:
                    source, blocks[k] = after((source, blocks[k]))
            result = held[v] = {k: gy.send(blocks[k], k) for k in blocks}
        else:
            term = Y_TERM.get(v)
            lines = [held[v][k] for k in range(1, gy.size)]
            term_lines = [] if term is None else [held[term][k] for k in range(1, gy.size)]
            whole = y_part(fields, place, v, lines, term, term_lines, matrices, scale_y)
            going = {k: whole[k] for k in step_order(gy.size)}
            if behind is not None:
                going, _ = after((going, behind))
            if v == AFTER_REST:
                going, rest = after((going, rest))
            if v == AFTER_FIRST:
                finished = [Y_ITEMS[4][1]]
                total = finish_variable(total, finished[0])
                going, total = after((going, total))
            result = {k: gy.send(going[k], k) for k in going}
            parts[v] = [whole[0]] + [result[k] for k in range(1, gy.size)]
        done.append(result)
    for kind, v in Y_ITEMS:
        if kind == "out" and v not in finished:
            total = finish_variable(total, v)
    return total


def step_order(size):
    half = size // 2
    return list(range(half, size)) + list(range(1, half))


def solution(mesh):
    return jax.shard_map(
        on_device,
        mesh=mesh,
        in_specs=(
            P(None, "src", "gy", "gx"),
            P(("gy", "gx"), None),
            P(),
            P(),
            P("gx"),
            P("gy"),
            P("src"),
            P("src", "gy"),
            P(("src", "gy", "gx"), None, None),
            P(("src", "gy", "gx")),
            P(("src", "gy", "gx"), None),
        ),
        out_specs=P(None, "src", "gy", "gx"),
        check_vma=False,
    )
```

```python
import jax
import jax.numpy as jnp
from jax import lax
from jax.experimental import pallas as pl
from jax.experimental.pallas import tpu as pltpu
from jax.sharding import PartitionSpec as P


ROW_LEN = 256
CAP = 2
DIGIT = 128
SLAB = 16
STEP_SIZE = 0.25
Y_ITEMS = (
    ("in", 2),
    ("in", 0),
    ("in", 4),
    ("in", 1),
    ("out", 0),
    ("in", 3),
    ("out", 2),
    ("out", 4),
    ("out", 1),
    ("out", 3),
)
IN_FLIGHT = 4
AFTER_REST = 1
AFTER_FIRST = 3
Y_TERM = {0: 2, 2: 4, 4: 2}


class Axis:
    def __init__(self, name):
        self.name = name
        self.size = lax.axis_size(name)
        self.me = lax.axis_index(name)
        self.xor = self.size & (self.size - 1) == 0

    def dest(self, k):
        return jnp.bitwise_xor(self.me, k) if self.xor else (self.me + k) % self.size

    def source(self, k):
        return jnp.bitwise_xor(self.me, k) if self.xor else (self.me - k) % self.size

    def send(self, array, k):
        pairs = [(i, i ^ k if self.xor else (i + k) % self.size) for i in range(self.size)]
        return lax.ppermute(array, self.name, pairs)

    def gather(self, array):
        return [array] + [self.send(array, k) for k in range(1, self.size)]

    def steps(self):
        return jnp.arange(self.size, dtype=jnp.int32)

    def in_place_order(self, pieces):
        return jnp.take(jnp.stack(pieces), self.source(self.steps()), axis=0)


def cost(flops, bytes_accessed):
    return pl.CostEstimate(flops=int(flops), transcendentals=0, bytes_accessed=int(bytes_accessed))


def largest_divisor(extent, most):
    return max(d for d in range(1, min(extent, most) + 1) if extent % d == 0)


def y_part(fields, place, variable, arrived, term, term_arrived, matrices, scale):
    num = len(arrived) + 1
    planes, rows, cells = arrived[0].shape
    zb = largest_divisor(planes, 4)
    per = planes // zb
    extent = num * rows
    full = jax.ShapeDtypeStruct(arrived[0].shape, jnp.bfloat16)
    groups = [(variable, arrived)] + ([] if term is None else [(term, term_arrived)])
    total = num * len(groups)

    def kernel(place_ref, *refs):
        mats_ref, scale_ref = refs[total : total + 2]
        out_refs = refs[total + 2 :]

        def product(group, matrix, z):
            first, *others = refs[group * num : (group + 1) * num]
            lines = jnp.concatenate([first[0, z]] + [r[z] for r in others], axis=0)
            return jnp.dot(mats_ref[matrix], lines, preferred_element_type=jnp.float32)

        for z in range(zb):
            acc = product(0, 1, z)
            if term is not None:
                acc += scale_ref[...] * product(1, 0, z)
            for k in range(num):
                out_refs[k][z] = acc[k * rows : (k + 1) * rows].astype(jnp.bfloat16)

    def own_place(v):
        return lambda i, p: (v, p[0] * per + i, 0, 0)

    block = pl.BlockSpec((zb, rows, cells), lambda i, p: (i, 0, 0))
    in_specs = []
    operands = []
    for v, blocks in groups:
        in_specs += [pl.BlockSpec((1, zb, rows, cells), own_place(v))] + [block] * (num - 1)
        operands += [fields] + list(blocks)
    in_specs += [
        pl.BlockSpec((2, extent, extent), lambda i, p: (0, 0, 0)),
        pl.BlockSpec((extent, 1), lambda i, p: (0, 0)),
    ]
    return pl.pallas_call(
        kernel,
        grid_spec=pltpu.PrefetchScalarGridSpec(
            num_scalar_prefetch=1, grid=(per,), in_specs=in_specs, out_specs=[block] * num
        ),
        out_shape=[full] * num,
        cost_estimate=cost(
            2 * extent * extent * planes * cells * len(groups),
            2 * extent * planes * cells * (len(groups) + 1),
        ),
    )(place, *operands, matrices, scale)


def z_part(fields, arrived, operator, scale):
    _, planes, rows, cells = fields.shape
    num = len(arrived) + 1
    slab = largest_divisor(rows, SLAB)
    size = planes * slab

    def kernel(own_ref, *refs):
        in_refs = (own_ref,) + refs[: num - 1]
        op_ref, scale_ref, out_ref = refs[num - 1 :]
        acc = jnp.zeros((size, cells), jnp.float32)
        for k in range(num):
            acc += jnp.dot(op_ref[k], in_refs[k][0].reshape(size, cells), preferred_element_type=jnp.float32)
        out_ref[0] = (scale_ref[...] * acc).reshape(planes, slab, cells).astype(jnp.bfloat16)

    block = (1, planes, slab, cells)
    here = pl.BlockSpec(block, lambda a, i: (a, 0, i, 0))
    return pl.pallas_call(
        kernel,
        grid=(2, rows // slab),
        in_specs=[pl.BlockSpec(block, lambda a, i: (a + 3, 0, i, 0))]
        + [here] * (num - 1)
        + [
            pl.BlockSpec((num, size, size), lambda a, i: (0, 0, 0)),
            pl.BlockSpec((size, 1), lambda a, i: (0, 0)),
        ],
        out_specs=here,
        out_shape=jax.ShapeDtypeStruct((2, planes, rows, cells), jnp.bfloat16),
        name="z_part",
        cost_estimate=cost(
            4 * num * size * size * cells * (rows // slab), 4 * (num + 1) * planes * rows * cells
        ),
    )(fields, *arrived, operator, scale)


def x_part(fields, arrived, operator, scale_x, speed, z_terms, rows_in, targets):
    num_vars, planes, rows, cells = fields.shape
    num = len(arrived) + 1
    zb = largest_divisor(planes, max(1, 256 // rows))
    size = zb * rows
    num_rows = targets.shape[0]
    width = min(ROW_LEN, cells)

    def kernel(targets_ref, own_ref, *refs):
        in_refs = (own_ref,) + refs[: num - 1]
        op_ref, scale_ref, speed_ref, z_ref, rows_ref, out_ref = refs[num - 1 :]
        speed_col = speed_ref[...].reshape(size, 1)

        def slope(v):
            acc = jnp.dot(
                in_refs[0][v].reshape(size, cells), op_ref[0], preferred_element_type=jnp.float32
            )
            for k in range(1, num):
                acc += jnp.dot(
                    in_refs[k][v].reshape(size, cells), op_ref[k], preferred_element_type=jnp.float32
                )
            return acc * scale_ref[...]

        def z_term(a):
            return z_ref[a].reshape(size, cells).astype(jnp.float32)

        def put(v, value):
            out_ref[v] = (-STEP_SIZE * value).reshape(zb, rows, cells)

        slope_u = slope(1)
        slope_p = slope(4)
        divergence = slope_u + z_term(0)
        put(1, speed_col * slope_u + slope_p)
        put(4, speed_col * slope_p + divergence)
        put(0, speed_col * slope(0) + divergence)
        put(2, speed_col * slope(2))
        put(3, speed_col * slope(3) + z_term(1))
        first = pl.program_id(0) * zb

        @pl.loop(0, num_rows)
        def _(r):
            for piece in range(ROW_LEN // width):
                cell = targets_ref[r] * ROW_LEN + piece * width
                plane = cell // (rows * cells) - first

                @pl.when((plane >= 0) & (plane < zb))
                def _():
                    row = (cell // cells) % rows
                    start = pl.multiple_of(cell % cells, width)
                    for v in range(num_vars):
                        place = (v, plane, pl.ds(row, 1), pl.ds(start, width))
                        out_ref[place] += rows_ref[r, v : v + 1, piece * width : (piece + 1) * width]

    block = pl.BlockSpec((num_vars, zb, rows, cells), lambda i, t: (0, i, 0, 0))
    return pl.pallas_call(
        kernel,
        grid_spec=pltpu.PrefetchScalarGridSpec(
            num_scalar_prefetch=1,
            grid=(planes // zb,),
            in_specs=[block] * num
            + [
                pl.BlockSpec((num, cells, cells), lambda i, t: (0, 0, 0)),
                pl.BlockSpec((1, cells), lambda i, t: (0, 0)),
                pl.BlockSpec((zb, rows, 1), lambda i, t: (i, 0, 0)),
                pl.BlockSpec((2, zb, rows, cells), lambda i, t: (0, i, 0, 0)),
                pl.BlockSpec(rows_in.shape, lambda i, t: (0, 0, 0)),
            ],
            out_specs=block,
        ),
        out_shape=jax.ShapeDtypeStruct(fields.shape, jnp.float32),
        name="x_part",
        cost_estimate=cost(
            2 * num_vars * planes * rows * cells * cells * num,
            num_vars * planes * rows * cells * (2 * num + 5),
        ),
    )(targets, fields, *arrived, operator, scale_x, speed, z_terms, rows_in)


def finish(total, rest, part, variable, place):
    planes, rows, cells = part.shape
    zb = largest_divisor(planes, 8)
    per = planes // zb

    def kernel(place_ref, rest_ref, part_ref, *refs):
        refs[-1][0] = (rest_ref[0] + part_ref[...].astype(jnp.float32)).astype(jnp.bfloat16)

    big = pl.BlockSpec((1, zb, rows, cells), lambda i, p: (variable, p[0] * per + i, 0, 0))
    in_specs = [big, pl.BlockSpec((zb, rows, cells), lambda i, p: (i, 0, 0))]
    operands = [rest, part]
    aliases = {}
    if total is not None:
        in_specs.append(pl.BlockSpec(memory_space=pl.ANY))
        operands.append(total)
        aliases = {3: 0}
    return pl.pallas_call(
        kernel,
        grid_spec=pltpu.PrefetchScalarGridSpec(
            num_scalar_prefetch=1, grid=(per,), in_specs=in_specs, out_specs=big
        ),
        out_shape=jax.ShapeDtypeStruct(rest.shape, jnp.bfloat16),
        input_output_aliases=aliases,
        cost_estimate=cost(planes * rows * cells, 8 * planes * rows * cells),
    )(place, *operands)


def route_rows(gy, gx, surface_rows, row_block, row_offsets, num_blocks):
    num_vars = surface_rows.shape[1]
    starts = row_offsets[0, :-1]
    counts = row_offsets[0, 1:] - starts
    slots = jnp.arange(CAP, dtype=jnp.int32)
    is_valid = slots[None, :] < counts[:, None]
    row_index = jnp.where(is_valid, starts[:, None] + slots[None, :], 0).reshape(-1)
    valid = is_valid.reshape(-1)[:, None]
    picked = jnp.take(surface_rows.reshape(-1, num_vars * ROW_LEN), row_index, axis=0)
    picked = jnp.where(valid, picked, jnp.zeros((), jnp.bfloat16))
    blocks = jnp.where(is_valid.reshape(-1), jnp.take(row_block, row_index), 0)
    digits = []
    scale = 1
    while scale < num_blocks:
        digits.append((blocks // scale) % DIGIT)
        scale *= DIGIT
    tail = jnp.stack(digits, axis=1).astype(jnp.bfloat16)
    tail = jnp.pad(tail, ((0, 0), (0, -len(digits) % 128)))
    packed = jnp.concatenate([picked, tail], axis=1).reshape(gy.size, gx.size, CAP, -1)
    for axis in (gy, gx):
        by_dest = [lax.dynamic_index_in_dim(packed, axis.dest(k), 0, keepdims=False) for k in range(axis.size)]
        got = [by_dest[0]] + [axis.send(by_dest[k], k) for k in range(1, axis.size)]
        packed = jnp.stack(got, axis=1) if axis is gy else jnp.stack(got)
    flat = packed.reshape(-1, packed.shape[-1])
    rows_in = flat[:, : num_vars * ROW_LEN].astype(jnp.float32).reshape(-1, num_vars, ROW_LEN)
    targets = jnp.zeros((flat.shape[0],), jnp.int32)
    for place in range(len(digits)):
        digit = flat[:, num_vars * ROW_LEN + place].astype(jnp.float32).astype(jnp.int32)
        targets += digit * DIGIT**place
    return rows_in, targets


def x_operator(src, gy, gx, dx_op):
    rows, extent = dx_op.shape
    cells = rows * gy.size
    share = rows // src.size if rows % src.size == 0 else rows
    split = share != rows
    piece = lax.dynamic_slice_in_dim(dx_op, src.me * share, share, 0) if split else dx_op
    columns = gy.in_place_order(gy.gather(piece))
    blocks = gx.in_place_order(gx.gather(columns)).swapaxes(0, 1)
    blocks = blocks.reshape(gy.size * gx.size, share, extent)
    needed = lax.dynamic_slice_in_dim(blocks, gx.me * gy.size, gy.size, 0)
    if split:
        needed = src.in_place_order(src.gather(needed)).swapaxes(0, 1)
    turned = needed.reshape(cells, extent).T.reshape(gx.size, cells, cells)
    return jnp.take(turned, gx.source(gx.steps()), axis=0)


def z_operator(src, dz_op, planes, slab):
    own = lax.dynamic_slice_in_dim(dz_op, src.me * planes, planes, 0)
    blocks = own.reshape(planes, src.size, planes).swapaxes(0, 1)
    blocks = jnp.take(blocks, src.source(src.steps()), axis=0)
    size = planes * slab
    index = jnp.arange(size, dtype=jnp.int32)
    spread = (index[:, None] // slab == jnp.arange(planes, dtype=jnp.int32)[None, :]).astype(jnp.bfloat16)
    same_row = (index[:, None] % slab) == (index[None, :] % slab)
    wide = jnp.einsum("pi,kij->kpj", spread, blocks, preferred_element_type=jnp.float32).astype(jnp.bfloat16)
    wide = jnp.einsum("kpj,qj->kpq", wide, spread, preferred_element_type=jnp.float32).astype(jnp.bfloat16)
    return jnp.where(same_row[None], wide, jnp.zeros((), jnp.bfloat16))


def y_operator(gy, y_ops, rows):
    num = y_ops.shape[0]
    blocks = y_ops.reshape(num, gy.size, rows, gy.size, rows)
    blocks = jnp.take(blocks, gy.dest(gy.steps()), axis=1)
    blocks = jnp.take(blocks, gy.source(gy.steps()), axis=3)
    return blocks.reshape(y_ops.shape)


def on_device(
    fields,
    dx_op,
    y_ops,
    dz_op,
    metric_x,
    metric_y,
    metric_z,
    mean_u,
    surface_rows,
    row_block,
    row_offsets,
):
    _, planes, rows, cells = fields.shape
    src, gy, gx = Axis("src"), Axis("gy"), Axis("gx")
    share = planes // gy.size

    after = lax.optimization_barrier
    place = gy.me.reshape(1).astype(jnp.int32)

    def z_block(array, v, k):
        return lax.dynamic_slice(array, (v, gy.dest(k) * share, 0, 0), (1, share, rows, cells))[0]

    matrices = y_operator(gy, y_ops, rows)
    metric_all = gy.in_place_order(gy.gather(metric_y.reshape(1, rows)))
    scale_y = -STEP_SIZE * jnp.take(metric_all, gy.dest(gy.steps()), axis=0).reshape(-1, 1)
    slab = largest_divisor(rows, SLAB)
    z_scale = jnp.repeat(metric_z, slab).reshape(-1, 1)
    num_blocks = planes * rows * cells // ROW_LEN
    rows_in, targets = route_rows(gy, gx, surface_rows, row_block, row_offsets, num_blocks)
    turned = x_operator(src, gy, gx, dx_op)

    x_fields, *_ = after((fields, turned, rows_in))
    x_arrived = [gx.send(x_fields, k) for k in range(1, gx.size)]
    z_fields, _ = after((fields, turned))
    z_arrived = [src.send(z_fields[3:5], k) for k in range(1, src.size)]
    z_terms = z_part(fields, z_arrived, z_operator(src, dz_op, planes, slab), z_scale)
    rest = x_part(
        fields,
        x_arrived,
        turned,
        metric_x.reshape(1, cells),
        mean_u.reshape(planes, rows, 1),
        z_terms,
        rows_in,
        targets,
    )

    def finish_variable(total, v):
        for k in range(gy.size):
            at = gy.source(k).reshape(1).astype(jnp.int32)
            total = finish(total, rest, parts[v][k], v, at)
        return total

    held, parts, done = {}, {}, []
    total = None
    finished = []
    blocks = None
    for kind, v in Y_ITEMS:
        behind = done[-IN_FLIGHT] if len(done) >= IN_FLIGHT else None
        if kind == "in":
            source = fields
            if behind is not None or blocks is not None:
                source, _ = after((fields, blocks if behind is None else behind))
            blocks = {}
            for k in step_order(gy.size, (kind, v)):
                blocks[k] = z_block(source, v, k)
                if not done and len(blocks) == 1:
                    source, blocks[k] = after((source, blocks[k]))
            result = held[v] = {k: gy.send(blocks[k], k) for k in blocks}
        else:
            term = Y_TERM.get(v)
            lines = [held[v][k] for k in range(1, gy.size)]
            term_lines = [] if term is None else [held[term][k] for k in range(1, gy.size)]
            whole = y_part(fields, place, v, lines, term, term_lines, matrices, scale_y)
            going = {k: whole[k] for k in step_order(gy.size, (kind, v))}
            if behind is not None:
                going, _ = after((going, behind))
            if v == AFTER_REST:
                going, rest = after((going, rest))
            if v == AFTER_FIRST:
                finished = [Y_ITEMS[4][1]]
                total = finish_variable(total, finished[0])
                going, total = after((going, total))
            result = {k: gy.send(going[k], k) for k in going}
            parts[v] = [whole[0]] + [result[k] for k in range(1, gy.size)]
        done.append(result)
    for kind, v in Y_ITEMS:
        if kind == "out" and v not in finished:
            total = finish_variable(total, v)
    return total


def step_order(size, item):
    half = size // 2 if item == Y_ITEMS[0] else 1
    return list(range(half, size)) + list(range(1, half))


def solution(mesh):
    return jax.shard_map(
        on_device,
        mesh=mesh,
        in_specs=(
            P(None, "src", "gy", "gx"),
            P(("gy", "gx"), None),
            P(),
            P(),
            P("gx"),
            P("gy"),
            P("src"),
            P("src", "gy"),
            P(("src", "gy", "gx"), None, None),
            P(("src", "gy", "gx")),
            P(("src", "gy", "gx"), None),
        ),
        out_specs=P(None, "src", "gy", "gx"),
        check_vma=False,
    )
```
